32 devices in a mesh: mem: 4 (over x, core), grid: 8 (over z, y).
Axes of the slice: x: 2, y: 2, z: 4, core: 2. Of those that a mesh axis runs over, the one named last changes fastest.
Arguments:
- obs_ensemble: bfloat16 [256, 32, 256], P('mem', 'grid'), may hold values from -6 to 6
- obs_values: bfloat16 [32, 256], P('grid'), may hold values from -6 to 6
- inverse_error: bfloat16 [32, 256], P('grid'), may hold values from 0.5 to 8
- obs_counts: int32 [32], P('grid'), may hold values from 1 to 256, as said below
- loc_offsets: int32 [32, 4], P('grid'), may hold values from -2 to 2, as said below
- background: bfloat16 [256, 256, 320], P('mem', 'grid'), may hold values from -6 to 6
Outputs:
- analysis: bfloat16 [256, 256, 320], P('mem', 'grid')
The draws below stay inside these ranges and needn't reach their ends.
Inputs may be any that keep to these rules, and one draw needn't show every extreme that they name: `obs_counts`: counts up to about five times their mean; some block in every draw is full. `loc_offsets`: entry 0 of every list is 0 (the block's own observations); the other entries of a list are distinct nonzero offsets.
All inputs are finite; a program needn't handle non-finite values.
Results may differ from the reference program's by a relative error of at most 0.0063.
Values may be sent and summed in bfloat16 or wider, within the bound.
A program may use at most 128 MiB of HBM per device.

```python
import math
import jax
import jax.numpy as jnp
from jax import lax

MEMBERS = 256
VARS = 320
BLOCK_COLS = 8
OBS_SLOTS = 256
REACH = 2
LOC_LEN = 4
NS_STEPS = 6
BLOCKS = 32
COLS = 256


def draw_obs_counts(key, part):
    first, second, third, fourth = jax.random.split(jax.random.fold_in(key, 11), 4)
    light = jax.random.randint(first, (BLOCKS,), 1, OBS_SLOTS // 4 + 1)
    heavy_pick = jax.random.randint(second, (BLOCKS,), 0, 8) == 0
    heavy = jax.random.randint(third, (BLOCKS,), OBS_SLOTS // 2, OBS_SLOTS + 1)
    counts = jnp.where(heavy_pick, heavy, light)
    full_block = jax.random.randint(fourth, (), 0, BLOCKS)
    counts = jnp.where(jnp.arange(BLOCKS) == full_block, OBS_SLOTS, counts)
    return counts.astype(jnp.int32)


def draw_loc_offsets(key, part):
    nonzero = jnp.concatenate([jnp.arange(-REACH, 0), jnp.arange(1, REACH + 1)]).astype(jnp.int32)
    dropped = jax.random.randint(jax.random.fold_in(key, 23), (BLOCKS,), 0, 2 * REACH)
    dropped = jnp.where(jnp.arange(BLOCKS) == 0, REACH, dropped)
    ranks = jnp.arange(2 * REACH - 1)
    kept = jnp.where(ranks[None, :] < dropped[:, None], nonzero[ranks][None, :], nonzero[ranks + 1][None, :])
    own = jnp.zeros((BLOCKS, 1), jnp.int32)
    return jnp.concatenate([own, kept.astype(jnp.int32)], axis=1).astype(jnp.int32)


def block_scale(own_key, extent, cuts, least, largest):
    loudness = 1.0
    for position, blocks in cuts:
        steps = jax.random.uniform(jax.random.fold_in(jax.random.fold_in(own_key, 6), position), (blocks,), jnp.float32, least / len(cuts), largest / len(cuts))
        loudness = loudness * jnp.repeat(jnp.exp(steps), extent[position] // blocks).reshape((-1,) + (1,) * (len(extent) - 1 - position))
    return loudness


def centred(key, dims, scale, bound, cuts=(), kind=jnp.bfloat16):
    loudness = block_scale(key, dims, cuts, -0.22, 0.18) if cuts else 1.0
    array = jax.random.normal(key, dims, jnp.float32) * scale * loudness
    return jnp.minimum(jnp.maximum(array, -bound), bound).astype(kind)


def setup_inputs(seed: int = 0) -> dict:
    keys = jax.random.split(jax.random.key(seed), 7)
    obs_ensemble = centred(keys[0], (MEMBERS, BLOCKS, OBS_SLOTS), 1.0, 6.0, ((0, 4), (1, 8)))
    obs_values = centred(keys[1], (BLOCKS, OBS_SLOTS), 1.0, 6.0, ((0, 8),))
    inverse_error = jnp.clip(jnp.exp(math.log(8.0) - 2.7725887 * jax.random.uniform(keys[2], (BLOCKS, OBS_SLOTS), jnp.float32) ** block_scale(keys[2], (BLOCKS, OBS_SLOTS), ((0, 8),), -0.2, 0.2)), 0.5, 8.0).astype(jnp.bfloat16)
    obs_counts = draw_obs_counts(jax.random.fold_in(keys[6], 71), 0)
    loc_offsets = draw_loc_offsets(jax.random.fold_in(keys[6], 71), 0)
    background = centred(keys[5], (MEMBERS, COLS, VARS), 1.0, 6.0, ((0, 4), (1, 8)))
    return dict(obs_ensemble=obs_ensemble, obs_values=obs_values, inverse_error=inverse_error, obs_counts=obs_counts, loc_offsets=loc_offsets, background=background)


def taper_of(offsets):
    return 1.0 / (1.0 + jnp.abs(offsets).astype(jnp.float32))

def block_weights(members, obs_row, weight_row):
    members_wide = members.astype(jnp.float32)
    obs_mean = lax.optimization_barrier(jnp.mean(members_wide, axis=0))
    scaled = ((members_wide - obs_mean) * weight_row).astype(jnp.bfloat16)
    innovation = (obs_row - obs_mean) * weight_row
    gram = jnp.dot(scaled, scaled.T, preferred_element_type=jnp.float32)
    rhs = jnp.dot(scaled.astype(jnp.float32), innovation, precision=lax.Precision.HIGHEST)
    identity = jnp.eye(MEMBERS, dtype=jnp.float32)
    system = identity + gram / (MEMBERS - 1)
    scale = jnp.sqrt(jnp.sum(system * system))
    upper = system / scale
    lower = identity
    for step in range(NS_STEPS):
        middle = 0.5 * (3.0 * identity - jnp.dot(lower, upper, precision=lax.Precision.HIGHEST))
        upper = jnp.dot(upper, middle, precision=lax.Precision.HIGHEST)
        lower = jnp.dot(middle, lower, precision=lax.Precision.HIGHEST)
    root_inv = lower / jnp.sqrt(scale)
    inner = jnp.dot(root_inv, rhs, precision=lax.Precision.HIGHEST)
    shift = jnp.dot(root_inv, inner, precision=lax.Precision.HIGHEST) / (MEMBERS - 1)
    return (root_inv + shift[:, None]).astype(jnp.bfloat16)

def apply_block(weights, block_state):
    state_wide = block_state.astype(jnp.float32)
    state_mean = lax.optimization_barrier(jnp.mean(state_wide, axis=0))
    perturbation = (state_wide - state_mean).astype(jnp.bfloat16)
    product = lax.dot_general(weights, perturbation, (((0,), (0,)), ((), ())), preferred_element_type=jnp.float32)
    return (state_mean + product).astype(jnp.bfloat16)

def reference(obs_ensemble, obs_values, inverse_error, obs_counts, loc_offsets, background):
    slot_ids = jnp.arange(OBS_SLOTS, dtype=jnp.int32)
    masked_inverse = inverse_error.astype(jnp.float32) * (slot_ids[None, :] < obs_counts[:, None]).astype(jnp.float32)

    def one_block(block):
        offsets = lax.dynamic_index_in_dim(loc_offsets, block, 0, keepdims=False)
        chosen = ((block + offsets) % BLOCKS).astype(jnp.int32)
        members = jnp.take(obs_ensemble, chosen, axis=1).reshape(MEMBERS, LOC_LEN * OBS_SLOTS)
        obs_row = jnp.take(obs_values, chosen, axis=0).astype(jnp.float32).reshape(LOC_LEN * OBS_SLOTS)
        weight_row = (jnp.take(masked_inverse, chosen, axis=0) * taper_of(offsets)[:, None]).reshape(LOC_LEN * OBS_SLOTS)
        weights = block_weights(members, obs_row, weight_row)
        start = (block * BLOCK_COLS).astype(jnp.int32)
        block_state = lax.dynamic_slice_in_dim(background, start, BLOCK_COLS, 1).reshape(MEMBERS, BLOCK_COLS * VARS)
        return apply_block(weights, block_state)
    result = lax.map(one_block, jnp.arange(BLOCKS, dtype=jnp.int32))
    result = result.reshape(BLOCKS, MEMBERS, BLOCK_COLS, VARS).transpose(1, 0, 2, 3)
    return result.reshape(MEMBERS, COLS, VARS)
```

```python
import functools

import jax
import jax.numpy as jnp
from jax import lax
from jax.experimental import pallas as pl
from jax.experimental.pallas import tpu as pltpu
from jax.sharding import PartitionSpec as P

REACH = 2
NS_STEPS = 6
PIECES = 2
AHEAD = 2
HUB = 0
OWN = 4
AROUND = OWN + 2 * REACH
MESH = pl.DeviceIdType.MESH
NT = (((1,), (1,)), ((), ()))


def halves(a):
    high = a.astype(jnp.bfloat16)
    return high, (a - high.astype(jnp.float32)).astype(jnp.bfloat16)


def dot(a, b):
    left = jnp.concatenate([a[0], a[0], a[1]], axis=1)
    right = jnp.concatenate([b[0], b[1], b[0]], axis=0)
    return jnp.dot(left, right, preferred_element_type=jnp.float32)


def kernel(n, grid_n, loc_ref, counts_ref, obs_ref, values_ref, inverse_ref, bg_ref, result,
           obs_in, values_in, inverse_in, mine, near, own_table, tables, raw, state, sent_w, got_w,
           group_sem, cross_sem, in_sem, obs_send, obs_pass, edge_send, obs_recv, tab_send, tab_recv, raw_sem,
           direct_send, pair_send, pass_send, state_recv, w_send, w_recv):
    me = lax.axis_index("mem")
    row = lax.axis_index("grid")
    core = lax.rem(me, 2)
    chip = me // 2
    side = lax.rem(chip, 2)
    pair = chip // 2
    sibling = me + 1 - 2 * core
    far = me + 2 - 4 * side
    rest = n // 2
    pairs = rest // 2
    relay = pairs == 1
    local, blocks, slots = obs_ref.shape
    cols, variables = bg_ref.shape[1:]
    members = n * local
    loc_len = loc_ref.shape[1]
    per = cols // blocks
    width = cols * variables
    chunks = PIECES * blocks
    step = width // chunks

    def at(mem, shift):
        return {"mem": mem, "grid": lax.rem(row + shift + grid_n, grid_n)}

    def rows_of(mem):
        return pl.ds(pl.multiple_of(mem * local, local), local)

    barrier = pltpu.get_barrier_semaphore()
    for p in range(n):
        if p != HUB:
            @pl.when(me != p)
            def _():
                pl.semaphore_signal(barrier, inc=1, device_id=at(p, 0), device_id_type=MESH)

    inputs = [pltpu.make_async_copy(source, target, in_sem.at[k]) for k, (source, target) in enumerate(
        ((obs_ref, obs_in), (values_ref, values_in), (inverse_ref, inverse_in)))]
    for copy in inputs:
        copy.start()

    def raw_copy(b):
        part = pl.ds(b * per, per)
        return pltpu.make_async_copy(bg_ref.at[:, part], raw.at[:, part], raw_sem.at[b])

    for b in range(blocks):
        raw_copy(b).start()
    own_rows = rows_of(me)
    inputs[0].wait()
    mine[...] = jnp.swapaxes(obs_in[...].astype(jnp.float32), 0, 1).astype(jnp.bfloat16)

    @pl.when(me != HUB)
    def _():
        pl.semaphore_wait(barrier, n - 1)
        pl.semaphore_signal(group_sem, inc=1, device_id=at(HUB, 0), device_id_type=MESH)

    @pl.when(me == HUB)
    def _():
        pl.semaphore_wait(group_sem, n - 1)
        for move in (-1, 1):
            pl.semaphore_signal(barrier, inc=1, device_id=at(HUB, move), device_id_type=MESH)

    def chip_of(i, t):
        return 2 * (i // OWN) + t

    def place_of(i):
        return i % OWN + REACH

    def obs_copy(i, t):
        return pltpu.make_async_remote_copy(
            src_ref=mine.at[i], dst_ref=near.at[place_of(i), own_rows],
            send_sem=obs_send.at[i, t], recv_sem=obs_recv.at[place_of(i), me],
            device_id=at(2 * chip_of(i, t) + core, 0), device_id_type=MESH)

    def obs_kept(i):
        return pltpu.make_async_copy(mine.at[i], near.at[place_of(i), own_rows], obs_recv.at[place_of(i), me])

    def obs_shared(i):
        return pltpu.make_async_remote_copy(
            src_ref=mine.at[i], dst_ref=near.at[place_of(i), own_rows],
            send_sem=obs_pass.at[place_of(i), 0], recv_sem=obs_recv.at[place_of(i), me],
            device_id=at(sibling, 0), device_id_type=MESH)

    def obs_passed(u, k):
        source = lax.rem(me + 2 * k, n)
        rows = rows_of(source)
        return pltpu.make_async_remote_copy(
            src_ref=near.at[u, rows], dst_ref=near.at[u, rows],
            send_sem=obs_pass.at[u, k], recv_sem=obs_recv.at[u, source],
            device_id=at(sibling, 0), device_id_type=MESH)

    def await_obs(u, mem):
        ref = near.at[u, rows_of(mem)]
        pltpu.make_async_copy(ref, ref, obs_recv.at[u, mem]).wait()

    def edge_of(i):
        upper = i % OWN >= REACH
        p = i // OWN + (1 if upper else -1)
        u = i % OWN - REACH if upper else i % OWN + OWN + REACH
        return p % pairs, p // pairs, u, 0 if upper else 1

    def edge_copy(i, t, source_ref, member):
        p, shift, u, c = edge_of(i)
        target = 2 * (2 * p + (side if relay else t)) + c
        return target, shift, lambda: pltpu.make_async_remote_copy(
            src_ref=source_ref, dst_ref=near.at[u, rows_of(member)],
            send_sem=edge_send.at[i, t], recv_sem=obs_recv.at[u, member],
            device_id=at(target, shift), device_id_type=MESH)

    def own_edge(i, t):
        return edge_copy(i, t, mine.at[i], me)

    def far_edge(i):
        return edge_copy(i, 1, near.at[place_of(i), rows_of(far)], far)[2]

    def edge_kept(i):
        u = edge_of(i)[2]
        return pltpu.make_async_copy(mine.at[i], near.at[u, own_rows], obs_recv.at[u, me])

    def table_copy(move):
        source, place = (blocks - REACH, 0) if move == 1 else (0, REACH + blocks)
        return pltpu.make_async_remote_copy(
            src_ref=own_table.at[pl.ds(source, REACH)], dst_ref=tables.at[pl.ds(place, REACH)],
            send_sem=tab_send.at[(move + 1) // 2], recv_sem=tab_recv.at[(move + 1) // 2],
            device_id=at(me, move), device_id_type=MESH)

    edge_sides = (0,) if relay else (0, 1)
    for i in range(blocks):
        for t in (0, 1):
            @pl.when(chip != chip_of(i, t))
            def _():
                obs_copy(i, t).start()

            @pl.when(chip == chip_of(i, t))
            def _():
                obs_kept(i).start()
                obs_shared(i).start()
        for t in edge_sides:
            target, shift, copy = own_edge(i, t)
            if shift == 0:
                @pl.when(me != target)
                def _():
                    copy().start()

                @pl.when(me == target)
                def _():
                    edge_kept(i).start()

    def piece(j):
        return pl.ds(j * step, step)

    def direct(k, j):
        part = state.at[own_rows, piece(j)]
        return pltpu.make_async_remote_copy(
            src_ref=part, dst_ref=part, send_sem=direct_send.at[k, j], recv_sem=state_recv.at[me, j],
            device_id=at(lax.rem(me + 2 * k, n), 0), device_id_type=MESH)

    def paired(j):
        part = state.at[own_rows, piece(j)]
        return pltpu.make_async_remote_copy(
            src_ref=part, dst_ref=part, send_sem=pair_send.at[j], recv_sem=state_recv.at[me, j],
            device_id=at(sibling, 0), device_id_type=MESH)

    def passed(k, j):
        source = lax.rem(me + n - 2 * k, n)
        part = state.at[rows_of(source), piece(j)]
        return pltpu.make_async_remote_copy(
            src_ref=part, dst_ref=part, send_sem=pass_send.at[k, j], recv_sem=state_recv.at[source, j],
            device_id=at(sibling, 0), device_id_type=MESH)

    def await_state(source, j):
        ref = state.at[rows_of(source), piece(j)]
        pltpu.make_async_copy(ref, ref, state_recv.at[source, j]).wait()

    def pass_on(j):
        for k in range(1, rest):
            await_state(lax.rem(me + n - 2 * k, n), j)
            passed(k, j).start()

    def flatten(b):
        raw_copy(b).wait()
        state[own_rows, b * per * variables : (b + 1) * per * variables] = (
            raw[:, b * per : (b + 1) * per].reshape(local, per * variables))
        for j in range(b * PIECES, (b + 1) * PIECES):
            for k in range(1, rest):
                direct(k, j).start()
            paired(j).start()

    flatten(0)
    inputs[1].wait()
    inputs[2].wait()
    values = values_in[...].astype(jnp.float32)
    inverse = inverse_in[...].astype(jnp.float32)
    lane = lax.broadcasted_iota(jnp.int32, (1, slots), 1)
    upmost = lax.broadcasted_iota(jnp.int32, (8, slots), 0) == 0
    for b in range(blocks):
        masked = jnp.where(lane < counts_ref[b], inverse[b : b + 1], 0.0)
        entry = jnp.where(upmost, values[b : b + 1], masked)
        own_table[b] = entry
        tables[REACH + b] = entry

    @pl.when(me == HUB)
    def _():
        pl.semaphore_wait(barrier, 2)
        for p in range(n):
            if p != HUB:
                pl.semaphore_signal(cross_sem, inc=1, device_id=at(p, 0), device_id_type=MESH)

    @pl.when(me != HUB)
    def _():
        pl.semaphore_wait(cross_sem, 1)

    for i in range(blocks):
        for t in edge_sides:
            _, shift, copy = own_edge(i, t)
            if shift != 0:
                copy().start()
    for move in (-1, 1):
        table_copy(move).start()
    for b in range(1, blocks):
        flatten(b)

    for u in range(REACH, REACH + OWN):
        for k in range(1, rest):
            await_obs(u, lax.rem(me + 2 * k, n))
            obs_passed(u, k).start()
        if relay:
            far_edge(u - REACH)().start()
    for u in range(REACH, REACH + OWN):
        await_obs(u, me)
        for k in range(rest):
            await_obs(u, 2 * k + 1 - core)

    def products(u):
        wide = near[u].astype(jnp.float32)
        table = tables[OWN * pair + u]
        mean = jnp.sum(wide, axis=0, keepdims=True) * (1.0 / members)
        scaled = ((wide - mean) * table[1:2]).astype(jnp.bfloat16)
        full = (table[0:1] - mean) * table[1:2]
        high = halves(full)
        low = (full - high[0].astype(jnp.float32) - high[1].astype(jnp.float32)).astype(jnp.bfloat16)
        place = lax.broadcasted_iota(jnp.int32, (16, slots), 0)
        lines = jnp.where(place == 0, high[0].astype(jnp.float32), jnp.where(
            place == 1, high[1].astype(jnp.float32), jnp.where(place == 2, low.astype(jnp.float32), 0.0)))
        left = jnp.concatenate([scaled, lines.astype(jnp.bfloat16)], axis=0)
        return lax.dot_general(left, scaled, NT, preferred_element_type=jnp.float32)

    totals = [jnp.zeros((members + 16, members), jnp.float32) for _ in range(2)]

    def add(u):
        found = products(u)
        for t in range(2):
            distance = u - REACH - 2 * core - t
            away = jnp.abs(distance)
            share = jnp.where(away == 0, 1.0, jnp.where(away == 1, 1.0 / 4.0, 1.0 / 9.0))
            taken = 0.0
            for j in range(loc_len):
                taken = taken + jnp.where(loc_ref[OWN * pair + 2 * core + t, j] == distance, share, 0.0)
            totals[t] = totals[t] + taken * found

    for u in range(REACH, REACH + OWN):
        add(u)
    for move in (-1, 1):
        table_copy(move).wait_recv()
    for e in range(REACH):
        u = e + (OWN + REACH) * core
        for source in range(n):
            await_obs(u, source)
        add(u)

    for j in range(AHEAD):
        pass_on(j)
    across = lax.broadcasted_iota(jnp.int32, (members, members), 0)
    along = lax.broadcasted_iota(jnp.int32, (members, members), 1)
    identity = (across == along).astype(jnp.float32)
    scales, uppers, lowers = [], [], []
    for t in range(2):
        system = identity + totals[t][:members] / (members - 1)
        square = jnp.sum(jnp.sum(system * system, axis=1, keepdims=True), axis=0, keepdims=True)
        scale = jnp.sqrt(square)
        first = system / scale
        middle = halves(1.5 * identity - 0.5 * first)
        scales.append(scale)
        uppers.append(halves(dot(halves(first), middle)))
        lowers.append(middle)
    for s in range(1, NS_STEPS):
        middles = [halves(1.5 * identity - 0.5 * dot(lowers[t], uppers[t])) for t in range(2)]
        if s < NS_STEPS - 1:
            uppers = [halves(dot(uppers[t], middles[t])) for t in range(2)]
            lowers = [halves(dot(middles[t], lowers[t])) for t in range(2)]
        else:
            roots = [dot(middles[t], lowers[t]) / jnp.sqrt(scales[t]) for t in range(2)]
    for t in range(2):
        root = halves(roots[t])
        lines = totals[t][members:]
        rhs = lines[0:1] + lines[1:2] + lines[2:3]
        rhs = jnp.broadcast_to(rhs, (16, members))
        shift = dot(halves(dot(halves(rhs), root)), root) / (members - 1)
        sent_w[t] = (roots[t] + shift[0:1]).astype(jnp.bfloat16)

    slot = OWN * pair + 2 * core

    def weight_copy(k):
        p, c = lax.rem(pair + k // 2, pairs), core if k % 2 == 0 else 1 - core
        peer = 4 * p + 2 * side + c
        return pltpu.make_async_remote_copy(
            src_ref=sent_w.at[:, rows_of(peer)], dst_ref=got_w.at[pl.ds(slot, 2)],
            send_sem=w_send.at[k], recv_sem=w_recv.at[me // 4, core], device_id=at(peer, 0), device_id_type=MESH)

    for k in range(1, 2 * pairs):
        weight_copy(k).start()
    pltpu.make_async_copy(sent_w.at[:, own_rows], got_w.at[pl.ds(slot, 2)], w_recv.at[pair, core]).start()
    for p in range(pairs):
        for c in range(2):
            part = got_w.at[pl.ds(OWN * p + 2 * c, 2)]
            pltpu.make_async_copy(part, part, w_recv.at[p, c]).wait()

    for b in range(blocks):
        weights = got_w[b].astype(jnp.float32)
        folded = weights - jnp.sum(weights, axis=1, keepdims=True) * (1.0 / members) + 1.0 / members
        both = jnp.concatenate(halves(folded), axis=0)
        parts = []
        for j in range(b * PIECES, (b + 1) * PIECES):
            if j + 1 < chunks and j + 1 >= AHEAD:
                pass_on(j + 1)
            await_state(sibling, j)
            for k in range(1, rest):
                await_state(lax.rem(sibling + n - 2 * k, n), j)
            total = jnp.dot(both, state[:, j * step : (j + 1) * step], preferred_element_type=jnp.float32)
            parts.append((total[:local] + total[local:]).astype(jnp.bfloat16))
        result[:, b * per : (b + 1) * per] = jnp.concatenate(parts, axis=1).reshape(local, per, variables)

    for i in range(blocks):
        for t in (0, 1):
            @pl.when(chip != chip_of(i, t))
            def _():
                obs_copy(i, t).wait_send()

            @pl.when(chip == chip_of(i, t))
            def _():
                obs_shared(i).wait_send()
        for t in edge_sides:
            target, shift, copy = own_edge(i, t)
            if shift == 0:
                @pl.when(me != target)
                def _():
                    copy().wait_send()
            else:
                copy().wait_send()
        if relay:
            far_edge(i)().wait_send()
    for u in range(REACH, REACH + OWN):
        for k in range(1, rest):
            obs_passed(u, k).wait_send()
    for move in (-1, 1):
        table_copy(move).wait_send()
    for k in range(1, 2 * pairs):
        weight_copy(k).wait_send()
    for j in range(chunks):
        paired(j).wait_send()
        for k in range(1, rest):
            direct(k, j).wait_send()
            passed(k, j).wait_send()


def spread(blocks, held_ref, out_ref, sems):
    per = out_ref.shape[1] // blocks
    parts = [pl.ds(b * per, per) for b in range(blocks)]
    copies = [pltpu.make_async_copy(held_ref.at[:, p], out_ref.at[:, p], sems.at[b]) for b, p in enumerate(parts)]
    for copy in copies:
        copy.start()
    for copy in copies:
        copy.wait()


def on_device(n, grid_n, obs_ensemble, obs_values, inverse_error, obs_counts, loc_offsets, background):
    local, blocks, slots = obs_ensemble.shape
    cols, variables = background.shape[1:]
    members = n * local
    width = cols * variables
    chunks = PIECES * blocks
    rest = n // 2
    assert blocks == n and n % 4 == 0
    dma = pltpu.SemaphoreType.DMA
    smem = pl.BlockSpec(memory_space=pltpu.SMEM)
    vmem = pl.BlockSpec(memory_space=pltpu.VMEM)
    whole = pl.BlockSpec(memory_space=pl.ANY)
    held = pl.pallas_call(
        functools.partial(kernel, n, grid_n),
        out_shape=pltpu.VMEM((local, cols, variables), jnp.bfloat16),
        in_specs=[smem, smem, whole, whole, whole, whole],
        out_specs=vmem,
        scratch_shapes=[
            pltpu.VMEM((local, blocks, slots), jnp.bfloat16),
            pltpu.VMEM((blocks, slots), jnp.bfloat16),
            pltpu.VMEM((blocks, slots), jnp.bfloat16),
            pltpu.VMEM((blocks, local, slots), jnp.bfloat16),
            pltpu.VMEM((AROUND, members, slots), jnp.bfloat16),
            pltpu.VMEM((blocks, 8, slots), jnp.float32),
            pltpu.VMEM((blocks + 2 * REACH, 8, slots), jnp.float32),
            pltpu.VMEM((local, cols, variables), jnp.bfloat16),
            pltpu.VMEM((members, width), jnp.bfloat16),
            pltpu.VMEM((2, members, members), jnp.bfloat16),
            pltpu.VMEM((n, local, members), jnp.bfloat16),
            pltpu.SemaphoreType.REGULAR,
            pltpu.SemaphoreType.REGULAR,
            dma((3,)),
            dma((blocks, 2)),
            dma((AROUND, rest)),
            dma((blocks, 2)),
            dma((AROUND, n)),
            dma((2,)),
            dma((2,)),
            dma((blocks,)),
            dma((rest, chunks)),
            dma((chunks,)),
            dma((rest, chunks)),
            dma((n, chunks)),
            dma((n,)),
            dma((rest // 2, 2)),
        ],
        compiler_params=pltpu.CompilerParams(collective_id=0, has_side_effects=True, vmem_limit_bytes=60 * 2**20),
        name="analysis",
    )(loc_offsets, obs_counts, obs_ensemble, obs_values, inverse_error, background)
    return pl.pallas_call(
        functools.partial(spread, blocks),
        out_shape=jax.ShapeDtypeStruct((local, cols, variables), jnp.bfloat16),
        in_specs=[vmem],
        out_specs=whole,
        scratch_shapes=[dma((blocks,))],
        compiler_params=pltpu.CompilerParams(vmem_limit_bytes=16 * 2**20),
        name="spread",
    )(held)


def solution(mesh):
    placed = (
        P("mem", "grid", None),
        P("grid", None),
        P("grid", None),
        P("grid"),
        P("grid", None),
        P("mem", "grid", None),
    )
    body = functools.partial(on_device, mesh.shape["mem"], mesh.shape["grid"])
    return jax.shard_map(body, mesh=mesh, in_specs=placed, out_specs=P("mem", "grid", None), check_vma=False)
```

```python
import functools

import jax
import jax.numpy as jnp
from jax import lax
from jax.experimental import pallas as pl
from jax.experimental.pallas import tpu as pltpu
from jax.sharding import PartitionSpec as P

REACH = 2
NS_STEPS = 6
AHEAD = 2
HUB = 0
OWN = 4
AROUND = OWN + 2 * REACH
MESH = pl.DeviceIdType.MESH
NT = (((1,), (1,)), ((), ()))


def halves(a):
    high = a.astype(jnp.bfloat16)
    return high, (a - high.astype(jnp.float32)).astype(jnp.bfloat16)


def dot(a, b):
    left = jnp.concatenate([a[0], a[0], a[1]], axis=1)
    right = jnp.concatenate([b[0], b[1], b[0]], axis=0)
    return jnp.dot(left, right, preferred_element_type=jnp.float32)


def cut(blocks, per):
    cuts = []
    for b in range(blocks):
        sizes = [per // 2, per // 2] if b + 1 < blocks else [per // 2, per // 4, per // 4]
        for size in sizes:
            cuts.append((cuts[-1][0] + cuts[-1][1] if cuts else 0, size))
    return cuts


def kernel(n, grid_n, loc_in, counts_in, obs_ref, values_ref, inverse_ref, bg_ref, result,
           loc_ref, counts_ref, obs_in, obs_far, values_in, inverse_in, mine, near, own_table, tables, raw, state, sent_w, got_w,
           group_sem, cross_sem, in_sem, far_send, far_recv, obs_send, obs_pass, edge_send, obs_recv, tab_send, tab_recv, raw_sem,
           direct_send, pair_send, pass_send, state_recv, w_send, w_recv):
    me = lax.axis_index("mem")
    row = lax.axis_index("grid")
    core = lax.rem(me, 2)
    chip = me // 2
    side = lax.rem(chip, 2)
    pair = chip // 2
    sibling = me + 1 - 2 * core
    far = me + 2 - 4 * side
    rest = n // 2
    pairs = rest // 2
    relay = pairs == 1
    local, blocks, slots = obs_ref.shape
    cols, variables = bg_ref.shape[1:]
    members = n * local
    loc_len = loc_in.shape[1]
    per = cols // blocks

    def at(mem, shift):
        return {"mem": mem, "grid": lax.rem(row + shift + grid_n, grid_n)}

    def rows_of(mem):
        return pl.ds(pl.multiple_of(mem * local, local), local)

    barrier = pltpu.get_barrier_semaphore()
    for p in range(n):
        if p != HUB:
            @pl.when(me != p)
            def _():
                pl.semaphore_signal(barrier, inc=1, device_id=at(p, 0), device_id_type=MESH)

    inputs = [pltpu.make_async_copy(source, target, in_sem.at[k]) for k, (source, target) in enumerate(
        ((obs_ref, obs_in), (values_ref, values_in), (inverse_ref, inverse_in), (loc_in, loc_ref), (counts_in, counts_ref)))]
    def raw_copy(b):
        part = pl.ds(b * per, per)
        return pltpu.make_async_copy(bg_ref.at[:, part], raw.at[:, part], raw_sem.at[b])

    raw_copy(0).start()
    for copy in inputs:
        copy.start()
    for b in range(1, blocks):
        raw_copy(b).start()
    own_rows = rows_of(me)

    def reordered(ref):
        return jnp.swapaxes(ref[...].astype(jnp.float32), 0, 1).astype(jnp.bfloat16)

    @pl.when(me != HUB)
    def _():
        pl.semaphore_wait(barrier, n - 1)
        pl.semaphore_signal(group_sem, inc=1, device_id=at(HUB, 0), device_id_type=MESH)

    @pl.when(me == HUB)
    def _():
        pl.semaphore_wait(group_sem, n - 1)
        for move in (-1, 1):
            pl.semaphore_signal(barrier, inc=1, device_id=at(HUB, move), device_id_type=MESH)

    far_copy = pltpu.make_async_remote_copy(
        src_ref=obs_ref, dst_ref=obs_far, send_sem=far_send, recv_sem=far_recv,
        device_id=at(far, 0), device_id_type=MESH)
    if relay:
        far_copy.start()

    def chip_of(i, t):
        return 2 * (i // OWN) + t

    def place_of(i):
        return i % OWN + REACH

    def obs_copy(i, t):
        return pltpu.make_async_remote_copy(
            src_ref=mine.at[i], dst_ref=near.at[place_of(i), own_rows],
            send_sem=obs_send.at[i, t], recv_sem=obs_recv.at[place_of(i), me],
            device_id=at(2 * chip_of(i, t) + core, 0), device_id_type=MESH)

    def obs_kept(i):
        return pltpu.make_async_copy(mine.at[i], near.at[place_of(i), own_rows], obs_recv.at[place_of(i), me])

    def obs_shared(i):
        return pltpu.make_async_remote_copy(
            src_ref=mine.at[i], dst_ref=near.at[place_of(i), own_rows],
            send_sem=obs_pass.at[place_of(i), 0], recv_sem=obs_recv.at[place_of(i), me],
            device_id=at(sibling, 0), device_id_type=MESH)

    def obs_passed(u, k):
        source = lax.rem(me + 2 * k, n)
        rows = rows_of(source)
        return pltpu.make_async_remote_copy(
            src_ref=near.at[u, rows], dst_ref=near.at[u, rows],
            send_sem=obs_pass.at[u, k], recv_sem=obs_recv.at[u, source],
            device_id=at(sibling, 0), device_id_type=MESH)

    def await_obs(u, mem):
        ref = near.at[u, rows_of(mem)]
        pltpu.make_async_copy(ref, ref, obs_recv.at[u, mem]).wait()

    def edge_of(i):
        upper = i % OWN >= REACH
        p = i // OWN + (1 if upper else -1)
        u = i % OWN - REACH if upper else i % OWN + OWN + REACH
        return p % pairs, p // pairs, u, 0 if upper else 1

    def edge_copy(i, t, source_ref, member):
        p, shift, u, c = edge_of(i)
        target = 2 * (2 * p + (side if relay else t)) + c
        return target, shift, lambda: pltpu.make_async_remote_copy(
            src_ref=source_ref, dst_ref=near.at[u, rows_of(member)],
            send_sem=edge_send.at[i, t], recv_sem=obs_recv.at[u, member],
            device_id=at(target, shift), device_id_type=MESH)

    def own_edge(i, t):
        return edge_copy(i, t, mine.at[i], me)

    def far_edge(i):
        return edge_copy(i, 1, near.at[place_of(i), rows_of(far)], far)[2]

    def edge_kept(i):
        u = edge_of(i)[2]
        return pltpu.make_async_copy(mine.at[i], near.at[u, own_rows], obs_recv.at[u, me])

    def table_copy(move):
        source, place = (blocks - REACH, 0) if move == 1 else (0, REACH + blocks)
        return pltpu.make_async_remote_copy(
            src_ref=own_table.at[pl.ds(source, REACH)], dst_ref=tables.at[pl.ds(place, REACH)],
            send_sem=tab_send.at[(move + 1) // 2], recv_sem=tab_recv.at[(move + 1) // 2],
            device_id=at(me, move), device_id_type=MESH)

    edge_sides = (0,) if relay else (0, 1)

    def send_obs():
        inputs[0].wait()
        mine[...] = reordered(obs_in)
        for i in range(blocks):
            if relay:
                obs_kept(i).start()
                obs_shared(i).start()
                continue
            for t in (0, 1):
                @pl.when(chip != chip_of(i, t))
                def _():
                    obs_copy(i, t).start()

                @pl.when(chip == chip_of(i, t))
                def _():
                    obs_kept(i).start()
                    obs_shared(i).start()
                target, shift, copy = own_edge(i, t)
                if shift == 0:
                    @pl.when(me != target)
                    def _():
                        copy().start()

                    @pl.when(me == target)
                    def _():
                        edge_kept(i).start()

    cuts = cut(blocks, per)
    chunks = len(cuts)
    pieces_of = [[j for j, (first, _) in enumerate(cuts) if first // per == b] for b in range(blocks)]

    def piece(j):
        return pl.ds(cuts[j][0] * variables, cuts[j][1] * variables)

    def direct(k, j):
        part = state.at[own_rows, piece(j)]
        return pltpu.make_async_remote_copy(
            src_ref=part, dst_ref=part, send_sem=direct_send.at[k, j], recv_sem=state_recv.at[me, j],
            device_id=at(lax.rem(me + 2 * k, n), 0), device_id_type=MESH)

    def paired(j):
        part = state.at[own_rows, piece(j)]
        return pltpu.make_async_remote_copy(
            src_ref=part, dst_ref=part, send_sem=pair_send.at[j], recv_sem=state_recv.at[me, j],
            device_id=at(sibling, 0), device_id_type=MESH)

    def passed(k, j):
        source = lax.rem(me + n - 2 * k, n)
        part = state.at[rows_of(source), piece(j)]
        return pltpu.make_async_remote_copy(
            src_ref=part, dst_ref=part, send_sem=pass_send.at[k, j], recv_sem=state_recv.at[source, j],
            device_id=at(sibling, 0), device_id_type=MESH)

    def await_state(source, j):
        ref = state.at[rows_of(source), piece(j)]
        pltpu.make_async_copy(ref, ref, state_recv.at[source, j]).wait()

    def pass_on(j):
        for k in range(1, rest):
            await_state(lax.rem(me + n - 2 * k, n), j)
            passed(k, j).start()

    def flatten(b):
        raw_copy(b).wait()
        state[own_rows, b * per * variables : (b + 1) * per * variables] = (
            raw[:, b * per : (b + 1) * per].reshape(local, per * variables))
        for j in pieces_of[b]:
            for k in range(1, rest):
                direct(k, j).start()
            paired(j).start()

    flatten(0)
    send_obs()
    for copy in inputs[1:]:
        copy.wait()
    values = values_in[...].astype(jnp.float32)
    inverse = inverse_in[...].astype(jnp.float32)
    lane = lax.broadcasted_iota(jnp.int32, (1, slots), 1)
    upmost = lax.broadcasted_iota(jnp.int32, (8, slots), 0) == 0
    for b in range(blocks):
        masked = jnp.where(lane < counts_ref[b], inverse[b : b + 1], 0.0)
        entry = jnp.where(upmost, values[b : b + 1], masked)
        own_table[b] = entry
        tables[REACH + b] = entry

    @pl.when(me == HUB)
    def _():
        pl.semaphore_wait(barrier, 2)
        for p in range(n):
            if p != HUB:
                pl.semaphore_signal(cross_sem, inc=1, device_id=at(p, 0), device_id_type=MESH)

    @pl.when(me != HUB)
    def _():
        pl.semaphore_wait(cross_sem, 1)

    for i in range(blocks):
        for t in edge_sides:
            _, shift, copy = own_edge(i, t)
            if shift != 0:
                copy().start()
    for move in (-1, 1):
        table_copy(move).start()
    for b in range(1, blocks):
        flatten(b)

    if relay:
        far_copy.wait_recv()
        near[REACH : REACH + OWN, rows_of(far)] = reordered(obs_far)
    for u in range(REACH, REACH + OWN):
        for k in range(1, rest):
            if not relay:
                await_obs(u, lax.rem(me + 2 * k, n))
            obs_passed(u, k).start()
        if relay:
            far_edge(u - REACH)().start()
    for u in range(REACH, REACH + OWN):
        await_obs(u, me)
        for k in range(rest):
            await_obs(u, 2 * k + 1 - core)

    def products(u):
        wide = near[u].astype(jnp.float32)
        table = tables[OWN * pair + u]
        mean = jnp.sum(wide, axis=0, keepdims=True) * (1.0 / members)
        scaled = ((wide - mean) * table[1:2]).astype(jnp.bfloat16)
        full = (table[0:1] - mean) * table[1:2]
        high = halves(full)
        low = (full - high[0].astype(jnp.float32) - high[1].astype(jnp.float32)).astype(jnp.bfloat16)
        place = lax.broadcasted_iota(jnp.int32, (16, slots), 0)
        lines = jnp.where(place == 0, high[0].astype(jnp.float32), jnp.where(
            place == 1, high[1].astype(jnp.float32), jnp.where(place == 2, low.astype(jnp.float32), 0.0)))
        left = jnp.concatenate([scaled, lines.astype(jnp.bfloat16)], axis=0)
        return lax.dot_general(left, scaled, NT, preferred_element_type=jnp.float32)

    totals = [jnp.zeros((members + 16, members), jnp.float32) for _ in range(2)]

    def add(u):
        found = products(u)
        for t in range(2):
            distance = u - REACH - 2 * core - t
            away = jnp.abs(distance)
            share = jnp.where(away == 0, 1.0, jnp.where(away == 1, 1.0 / 4.0, 1.0 / 9.0))
            taken = 0.0
            for j in range(loc_len):
                taken = taken + jnp.where(loc_ref[OWN * pair + 2 * core + t, j] == distance, share, 0.0)
            totals[t] = totals[t] + taken * found

    for u in range(REACH, REACH + OWN):
        add(u)
    for move in (-1, 1):
        table_copy(move).wait_recv()
    for e in range(REACH):
        u = e + (OWN + REACH) * core
        for source in range(n):
            await_obs(u, source)
        add(u)

    for j in range(AHEAD):
        pass_on(j)
    across = lax.broadcasted_iota(jnp.int32, (members, members), 0)
    along = lax.broadcasted_iota(jnp.int32, (members, members), 1)
    identity = (across == along).astype(jnp.float32)
    scales, uppers, lowers = [], [], []
    for t in range(2):
        system = identity + totals[t][:members] / (members - 1)
        square = jnp.sum(jnp.sum(system * system, axis=1, keepdims=True), axis=0, keepdims=True)
        scale = jnp.sqrt(square)
        first = system / scale
        middle = halves(1.5 * identity - 0.5 * first)
        scales.append(scale)
        uppers.append(halves(dot(halves(first), middle)))
        lowers.append(middle)
    for s in range(1, NS_STEPS):
        middles = [halves(1.5 * identity - 0.5 * dot(lowers[t], uppers[t])) for t in range(2)]
        if s < NS_STEPS - 1:
            uppers = [halves(dot(uppers[t], middles[t])) for t in range(2)]
            lowers = [halves(dot(middles[t], lowers[t])) for t in range(2)]
        else:
            roots = [dot(middles[t], lowers[t]) / jnp.sqrt(scales[t]) for t in range(2)]
    for t in range(2):
        root = halves(roots[t])
        lines = totals[t][members:]
        rhs = lines[0:1] + lines[1:2] + lines[2:3]
        rhs = jnp.broadcast_to(rhs, (16, members))
        shift = dot(halves(dot(halves(rhs), root)), root) / (members - 1)
        sent_w[t] = (roots[t] + shift[0:1]).astype(jnp.bfloat16)

    slot = OWN * pair + 2 * core

    def weight_copy(k):
        p, c = lax.rem(pair + k // 2, pairs), core if k % 2 == 0 else 1 - core
        peer = 4 * p + 2 * side + c
        return pltpu.make_async_remote_copy(
            src_ref=sent_w.at[:, rows_of(peer)], dst_ref=got_w.at[pl.ds(slot, 2)],
            send_sem=w_send.at[k], recv_sem=w_recv.at[me // 4, core], device_id=at(peer, 0), device_id_type=MESH)

    for k in range(1, 2 * pairs):
        weight_copy(k).start()
    pltpu.make_async_copy(sent_w.at[:, own_rows], got_w.at[pl.ds(slot, 2)], w_recv.at[pair, core]).start()
    for p in range(pairs):
        for c in range(2):
            part = got_w.at[pl.ds(OWN * p + 2 * c, 2)]
            pltpu.make_async_copy(part, part, w_recv.at[p, c]).wait()

    def settle():
        if relay:
            far_copy.wait_send()
        for i in range(blocks):
            for t in (0, 1):
                if relay:
                    continue
                @pl.when(chip != chip_of(i, t))
                def _():
                    obs_copy(i, t).wait_send()

                @pl.when(chip == chip_of(i, t))
                def _():
                    obs_shared(i).wait_send()
            if relay:
                obs_shared(i).wait_send()
                far_edge(i)().wait_send()
            for t in edge_sides:
                target, shift, copy = own_edge(i, t)
                if shift == 0:
                    @pl.when(me != target)
                    def _():
                        copy().wait_send()
                else:
                    copy().wait_send()
        for u in range(REACH, REACH + OWN):
            for k in range(1, rest):
                obs_passed(u, k).wait_send()
        for move in (-1, 1):
            table_copy(move).wait_send()
        for k in range(1, 2 * pairs):
            weight_copy(k).wait_send()
        for j in range(chunks):
            paired(j).wait_send()
            for k in range(1, rest):
                direct(k, j).wait_send()
                passed(k, j).wait_send()

    for b in range(blocks):
        weights = got_w[b].astype(jnp.float32)
        folded = weights - jnp.sum(weights, axis=1, keepdims=True) * (1.0 / members) + 1.0 / members
        both = jnp.concatenate(halves(folded), axis=0)
        parts = []
        for j in pieces_of[b]:
            if AHEAD <= j + 1 < chunks:
                pass_on(j + 1)
            if j == chunks - 1:
                settle()
            await_state(sibling, j)
            for k in range(1, rest):
                await_state(lax.rem(sibling + n - 2 * k, n), j)
            total = jnp.dot(both, state[:, piece(j)], preferred_element_type=jnp.float32)
            parts.append((total[:local] + total[local:]).astype(jnp.bfloat16))
        result[:, b * per : (b + 1) * per] = jnp.concatenate(parts, axis=1).reshape(local, per, variables)


def spread(blocks, held_ref, out_ref, sems):
    per = out_ref.shape[1] // blocks
    parts = [pl.ds(b * per, per) for b in range(blocks)]
    copies = [pltpu.make_async_copy(held_ref.at[:, p], out_ref.at[:, p], sems.at[b]) for b, p in enumerate(parts)]
    for copy in copies:
        copy.start()
    for copy in copies:
        copy.wait()


def on_device(n, grid_n, obs_ensemble, obs_values, inverse_error, obs_counts, loc_offsets, background):
    local, blocks, slots = obs_ensemble.shape
    cols, variables = background.shape[1:]
    members = n * local
    width = cols * variables
    chunks = len(cut(blocks, cols // blocks))
    rest = n // 2
    assert blocks == n and n % 4 == 0
    dma = pltpu.SemaphoreType.DMA
    vmem = pl.BlockSpec(memory_space=pltpu.VMEM)
    whole = pl.BlockSpec(memory_space=pl.ANY)
    held = pl.pallas_call(
        functools.partial(kernel, n, grid_n),
        out_shape=pltpu.VMEM((local, cols, variables), jnp.bfloat16),
        in_specs=[whole] * 6,
        out_specs=vmem,
        scratch_shapes=[
            pltpu.SMEM(loc_offsets.shape, jnp.int32),
            pltpu.SMEM(obs_counts.shape, jnp.int32),
            pltpu.VMEM((local, blocks, slots), jnp.bfloat16),
            pltpu.VMEM((local, blocks, slots), jnp.bfloat16),
            pltpu.VMEM((blocks, slots), jnp.bfloat16),
            pltpu.VMEM((blocks, slots), jnp.bfloat16),
            pltpu.VMEM((blocks, local, slots), jnp.bfloat16),
            pltpu.VMEM((AROUND, members, slots), jnp.bfloat16),
            pltpu.VMEM((blocks, 8, slots), jnp.float32),
            pltpu.VMEM((blocks + 2 * REACH, 8, slots), jnp.float32),
            pltpu.VMEM((local, cols, variables), jnp.bfloat16),
            pltpu.VMEM((members, width), jnp.bfloat16),
            pltpu.VMEM((2, members, members), jnp.bfloat16),
            pltpu.VMEM((n, local, members), jnp.bfloat16),
            pltpu.SemaphoreType.REGULAR,
            pltpu.SemaphoreType.REGULAR,
            dma((5,)),
            dma(()),
            dma(()),
            dma((blocks, 2)),
            dma((AROUND, rest)),
            dma((blocks, 2)),
            dma((AROUND, n)),
            dma((2,)),
            dma((2,)),
            dma((blocks,)),
            dma((rest, chunks)),
            dma((chunks,)),
            dma((rest, chunks)),
            dma((n, chunks)),
            dma((n,)),
            dma((rest // 2, 2)),
        ],
        compiler_params=pltpu.CompilerParams(collective_id=0, has_side_effects=True, vmem_limit_bytes=60 * 2**20),
        name="analysis",
    )(loc_offsets, obs_counts, obs_ensemble, obs_values, inverse_error, background)
    return pl.pallas_call(
        functools.partial(spread, blocks),
        out_shape=jax.ShapeDtypeStruct((local, cols, variables), jnp.bfloat16),
        in_specs=[vmem],
        out_specs=whole,
        scratch_shapes=[dma((blocks,))],
        compiler_params=pltpu.CompilerParams(vmem_limit_bytes=16 * 2**20),
        name="spread",
    )(held)


def solution(mesh):
    placed = (
        P("mem", "grid", None),
        P("grid", None),
        P("grid", None),
        P("grid"),
        P("grid", None),
        P("mem", "grid", None),
    )
    body = functools.partial(on_device, mesh.shape["mem"], mesh.shape["grid"])
    return jax.shard_map(body, mesh=mesh, in_specs=placed, out_specs=P("mem", "grid", None), check_vma=False)
```
